32 devices in a mesh: expert: 8 (over z, y), dp: 4 (over x, core).
Axes of the slice: x: 2, y: 2, z: 4, core: 2. Of those that a mesh axis runs over, the one named last changes fastest.
Arguments:
- tokens: bfloat16 [4096, 2048], P(('expert', 'dp')), may hold values from -6 to 6
- cotangent: bfloat16 [4096, 2048], P(('expert', 'dp')), may hold values from -3 to 3
- route_ids: int32 [4096, 2], P(('expert', 'dp')), may hold values from 0 to 8, as said below
- route_weights: float32 [4096, 2], P(('expert', 'dp')), may hold values from 0.2 to 1
- cold_gate: bfloat16 [8, 768, 2048], P('expert', 'dp'), may hold values from -0.125 to 0.125
- cold_up: bfloat16 [8, 768, 2048], P('expert', 'dp'), may hold values from -0.125 to 0.125
- cold_down: bfloat16 [8, 768, 2048], P('expert', 'dp'), may hold values from -0.21875 to 0.21875
- hot_gate: bfloat16 [1, 768, 2048], P(None, 'dp'), may hold values from -0.125 to 0.125
- hot_up: bfloat16 [1, 768, 2048], P(None, 'dp'), may hold values from -0.125 to 0.125
- hot_down: bfloat16 [1, 768, 2048], P(None, 'dp'), may hold values from -0.21875 to 0.21875
Outputs:
- mixed: bfloat16 [4096, 2048], P(('expert', 'dp'))
- token_grad: bfloat16 [4096, 2048], P(('expert', 'dp'))
- route_grad: float32 [4096, 2], P(('expert', 'dp'))
- cold_gate_grad: bfloat16 [8, 768, 2048], P('expert', 'dp')
- cold_up_grad: bfloat16 [8, 768, 2048], P('expert', 'dp')
- cold_down_grad: bfloat16 [8, 768, 2048], P('expert', 'dp')
- hot_gate_grad: float32 [1, 768, 2048], P(None, 'dp', 'expert')
- hot_up_grad: float32 [1, 768, 2048], P(None, 'dp', 'expert')
- hot_down_grad: float32 [1, 768, 2048], P(None, 'dp', 'expert')
The draws below stay inside these ranges and needn't reach their ends.
Inputs may be any that keep to these rules, and one draw needn't show every extreme that they name: `route_ids`: each row names 2 different experts. Experts 8 and above are the hot ones; among the rows of one device each hot expert is named exactly 32 times, no row names two hot experts, every other expert is named at most 36 times, and one expert below 8 is named exactly 36 times in the rows of every device.
All inputs are finite; a program needn't handle non-finite values.
Results may differ from the reference program's by a relative error of at most 0.014.
Values may be sent and summed in bfloat16 or wider, within the bound.
A program may use at most 128 MiB of HBM per device.

```python
import jax
import jax.numpy as jnp
from jax import lax

D = 2048
FF = 768
TOK_DEV = 128
TOP = 2
HOT = 1
COLD = 8
EXPERTS = 9
HOT_LOAD = 32
COLD_SLOTS = 224
CAP = 36
TOKENS = 4096
N_EXPERT = 8
N_DP = 4


def draw_route_ids(key, part):
    blocks = TOKENS // TOK_DEV
    pool_size = COLD * CAP
    key_full, key_rate, key_blocks = jax.random.split(jax.random.fold_in(key, 17), 3)
    full_expert = jax.random.randint(key_full, (), 0, COLD)
    expert_rates = jax.random.randint(key_rate, (COLD,), 0, 64)

    def one_block(block_key):
        key_base, key_order, key_turn = jax.random.split(block_key, 3)
        base_score = jax.random.randint(key_base, (pool_size,), 0, 256)
        slot_ids = jnp.arange(pool_size, dtype=jnp.int32)
        owner_ids = slot_ids // CAP
        slot_level = slot_ids % CAP
        scores = base_score + slot_level * expert_rates[owner_ids]
        scores = scores * pool_size + slot_ids
        scores = jnp.where(owner_ids == full_expert, slot_ids - pool_size, scores)
        neg_best, chosen = lax.top_k(-scores, COLD_SLOTS)
        cold_ids = (chosen // CAP).astype(jnp.int32)
        hot_ids = (COLD + jnp.arange(HOT * HOT_LOAD, dtype=jnp.int32) // HOT_LOAD).astype(jnp.int32)
        listing = jnp.sort(jnp.concatenate([cold_ids, hot_ids]))
        paired = listing.reshape(TOP, TOK_DEV).T
        turns = jax.random.randint(key_turn, (TOK_DEV, 1), 0, TOP)
        columns = (jnp.arange(TOP, dtype=jnp.int32)[None, :] + turns) % TOP
        paired = jnp.take_along_axis(paired, columns, axis=1)
        order = jax.random.permutation(key_order, TOK_DEV)
        return paired[order]
    block_keys = jax.random.split(key_blocks, blocks)
    return jax.vmap(one_block)(block_keys).reshape(TOKENS, TOP).astype(jnp.int32)


def strengthened(array, own_key, source, target, parts, factor):
    owner, partner = [(jnp.arange(array.shape[dim]) // (array.shape[dim] // parts)).reshape([-1 if axis == dim else 1 for axis in range(array.ndim)]) for dim in (source, target)]
    chosen = jax.random.permutation(own_key, parts)[partner]
    strong = (owner == chosen) | (owner == (partner + parts // 2) % parts)
    return jnp.where(strong, factor * array, array)


def block_levels(rng, dims, cuts, least, high):
    level = 1.0
    for dim, blocks in cuts:
        heights = jax.random.uniform(jax.random.fold_in(jax.random.fold_in(rng, 6), dim), (blocks,), jnp.float32, least / len(cuts), high / len(cuts))
        level = level * jnp.repeat(jnp.exp(heights), dims[dim] // blocks).reshape((-1,) + (1,) * (len(dims) - 1 - dim))
    return level


def centred(stream_key, extent, spread, reach, cuts=(), kind=jnp.bfloat16):
    values = jax.random.normal(stream_key, extent, jnp.float32) * spread
    if len(cuts) > 0:
        values = block_levels(stream_key, extent, cuts, -0.22, 0.18) * values
    return jnp.clip(values, min=-reach, max=reach).astype(kind)


def noise_with(stream_key, dims, deviation, bound, pieces, heavy, kind=jnp.bfloat16):
    values = deviation * jax.random.normal(stream_key, dims, jnp.float32)
    if pieces:
        values = values * block_levels(stream_key, dims, pieces, -0.22, 0.18)
    return jnp.clip(strengthened(values, jax.random.fold_in(stream_key, 3), *heavy), -bound, bound).astype(kind)


def setup_inputs(seed: int = 0) -> dict:
    seeds = jax.random.split(jax.random.key(seed), 11)
    tokens = noise_with(seeds[0], (TOKENS, D), 1.0, 6.0, ((0, 32),), (0, 1, 32, 2.75))
    cotangent = centred(seeds[1], (TOKENS, D), 0.5, 3.0, ((0, 32),))
    route_ids = draw_route_ids(jax.random.fold_in(seeds[10], 71), 0)
    route_weights = jnp.clip(0.2 + 0.8 * jax.random.uniform(seeds[3], (TOKENS, TOP), jnp.float32) ** block_levels(seeds[3], (TOKENS, TOP), ((0, 32),), -0.2, 0.2), 0.2, 1.0)
    cold_gate = centred(seeds[4], (COLD, FF, D), D ** -0.5, 0.125, ((0, 8), (1, 4)))
    cold_up = centred(seeds[5], (COLD, FF, D), D ** -0.5, 0.125, ((0, 8), (1, 4)))
    cold_down = centred(seeds[6], (COLD, FF, D), FF ** -0.5, 0.21875, ((0, 8), (1, 4)))
    hot_gate = centred(seeds[7], (HOT, FF, D), D ** -0.5, 0.125, ((1, 4),))
    hot_up = centred(seeds[8], (HOT, FF, D), D ** -0.5, 0.125, ((1, 4),))
    hot_down = centred(seeds[9], (HOT, FF, D), FF ** -0.5, 0.21875, ((1, 4),))
    return {"tokens": tokens, "cotangent": cotangent, "route_ids": route_ids, "route_weights": route_weights, "cold_gate": cold_gate, "cold_up": cold_up, "cold_down": cold_down, "hot_gate": hot_gate, "hot_up": hot_up, "hot_down": hot_down}


def expert_block(rows_x, rows_d, w_gate, w_up, w_down, grouped):
    count = rows_x.shape[0]
    quarter = w_gate.shape[0] // N_DP
    last_pair = (((1,), (1,)), ((), ()))
    pre_gate = lax.dot_general(rows_x, w_gate, last_pair, preferred_element_type=jnp.float32)
    pre_up = lax.dot_general(rows_x, w_up, last_pair, preferred_element_type=jnp.float32)
    sigma = jax.nn.sigmoid(pre_gate)
    act_full = pre_gate * sigma
    slope = sigma * (1.0 + pre_gate * (1.0 - sigma))
    act = (act_full * pre_up).astype(jnp.bfloat16)
    act_q = act.astype(jnp.float32).reshape(count, N_DP, quarter)
    down_q = w_down.astype(jnp.float32).reshape(N_DP, quarter, D)
    out_part = jnp.einsum("rqf,qfd->rqd", act_q, down_q).astype(jnp.bfloat16)
    out_part = lax.optimization_barrier(out_part)
    expert_out = jnp.sum(out_part.astype(jnp.float32), axis=1).astype(jnp.bfloat16)
    d_act = lax.dot_general(rows_d, w_down, last_pair, preferred_element_type=jnp.float32)
    d_gate = (d_act * pre_up * slope).astype(jnp.bfloat16)
    d_up = (d_act * act_full).astype(jnp.bfloat16)
    gate_q = w_gate.astype(jnp.float32).reshape(N_DP, quarter, D)
    up_q = w_up.astype(jnp.float32).reshape(N_DP, quarter, D)
    dg_q = d_gate.astype(jnp.float32).reshape(count, N_DP, quarter)
    du_q = d_up.astype(jnp.float32).reshape(count, N_DP, quarter)
    dx_part = (jnp.einsum("rqf,qfd->rqd", dg_q, gate_q) + jnp.einsum("rqf,qfd->rqd", du_q, up_q)).astype(jnp.bfloat16)
    dx_part = lax.optimization_barrier(dx_part)
    dx_pair = jnp.sum(dx_part.astype(jnp.float32), axis=1).astype(jnp.bfloat16)
    if grouped:
        xs = rows_x.astype(jnp.float32).reshape(N_DP, -1, D)
        ds = rows_d.astype(jnp.float32).reshape(N_DP, -1, D)
        dg = d_gate.astype(jnp.float32).reshape(N_DP, -1, w_gate.shape[0])
        du = d_up.astype(jnp.float32).reshape(N_DP, -1, w_gate.shape[0])
        av = act.astype(jnp.float32).reshape(N_DP, -1, w_gate.shape[0])
        part_gate = jnp.einsum("gpf,gpd->gfd", dg, xs).astype(jnp.bfloat16)
        part_up = jnp.einsum("gpf,gpd->gfd", du, xs).astype(jnp.bfloat16)
        part_down = jnp.einsum("gpf,gpd->gfd", av, ds).astype(jnp.bfloat16)
        part_gate, part_up, part_down = lax.optimization_barrier((part_gate, part_up, part_down))
        grad_gate = jnp.sum(part_gate.astype(jnp.float32), axis=0)
        grad_up = jnp.sum(part_up.astype(jnp.float32), axis=0)
        grad_down = jnp.sum(part_down.astype(jnp.float32), axis=0)
    else:
        grad_gate = jnp.dot(d_gate.T, rows_x, preferred_element_type=jnp.float32)
        grad_up = jnp.dot(d_up.T, rows_x, preferred_element_type=jnp.float32)
        grad_down = jnp.dot(act.T, rows_d, preferred_element_type=jnp.float32)
    return expert_out, dx_pair, grad_gate, grad_up, grad_down


def reference(tokens, cotangent, route_ids, route_weights, cold_gate, cold_up, cold_down, hot_gate, hot_up, hot_down):
    pair_count = TOKENS * TOP
    flat_ids = route_ids.reshape(pair_count).astype(jnp.int32)
    pair_gain = route_weights.reshape(pair_count)
    token_of = (jnp.arange(pair_count, dtype=jnp.int32) // TOP).astype(jnp.int32)
    group_of = ((token_of // TOK_DEV) % N_DP).astype(jnp.int32)
    pair_cot = (pair_gain[:, None] * cotangent[token_of].astype(jnp.float32)).astype(jnp.bfloat16)
    combo = (flat_ids * N_DP + group_of).astype(jnp.int32)
    onehot = (combo[:, None] == jnp.arange(EXPERTS * N_DP, dtype=jnp.int32)[None, :]).astype(jnp.int32)
    slot_rank = jnp.sum((jnp.cumsum(onehot, axis=0) - onehot) * onehot, axis=1).astype(jnp.int32)

    def run_group(first, count, per_group, w_gate, w_up, w_down, grouped):
        buffer = N_DP * per_group
        mine = (flat_ids >= first) & (flat_ids < first + count)
        position = jnp.where(mine, (flat_ids - first) * buffer + group_of * per_group + slot_rank, count * buffer).astype(jnp.int32)
        row_index = jnp.zeros((count * buffer + 1,), jnp.int32).at[position].set(jnp.arange(pair_count, dtype=jnp.int32))
        row_index = row_index[:count * buffer].reshape(count, buffer)
        live_mask = jnp.zeros((count * buffer + 1,), jnp.bool_).at[position].set(True)
        live_mask = live_mask[:count * buffer].reshape(count, buffer)

        def one_expert(expert_item):
            pair_index, live_rows, g_weight, u_weight, d_weight = expert_item
            picked_x = tokens[token_of[pair_index]]
            picked_d = pair_cot[pair_index]
            rows_x = jnp.where(live_rows[:, None], picked_x, jnp.zeros_like(picked_x))
            rows_d = jnp.where(live_rows[:, None], picked_d, jnp.zeros_like(picked_d))
            return expert_block(rows_x, rows_d, g_weight, u_weight, d_weight, grouped)

        results = lax.map(one_expert, (row_index, live_mask, w_gate, w_up, w_down))
        clipped = jnp.minimum(position, count * buffer - 1).astype(jnp.int32)
        outs_pair = results[0].reshape(count * buffer, D)[clipped]
        grads_pair = results[1].reshape(count * buffer, D)[clipped]
        return mine, outs_pair, grads_pair, results[2], results[3], results[4]

    cold_mine, cold_out, cold_dx, cg_grad, cu_grad, cd_grad = run_group(0, COLD, N_EXPERT * CAP, cold_gate, cold_up, cold_down, True)
    hot_mine, hot_out, hot_dx, hg_grad, hu_grad, hd_grad = run_group(COLD, HOT, N_EXPERT * HOT_LOAD, hot_gate, hot_up, hot_down, False)
    expert_out = jnp.where(cold_mine[:, None], cold_out, hot_out).reshape(TOKENS, TOP, D).astype(jnp.float32)
    dx_pair = jnp.where(cold_mine[:, None], cold_dx, hot_dx).reshape(TOKENS, TOP, D).astype(jnp.float32)
    mixed = jnp.sum(route_weights[:, :, None] * expert_out, axis=1).astype(jnp.bfloat16)
    route_grad = jnp.sum(cotangent.astype(jnp.float32)[:, None, :] * expert_out, axis=2)
    token_grad = jnp.sum(dx_pair, axis=1).astype(jnp.bfloat16)
    return (mixed, token_grad, route_grad, cg_grad.astype(jnp.bfloat16), cu_grad.astype(jnp.bfloat16), cd_grad.astype(jnp.bfloat16), hg_grad, hu_grad, hd_grad)
```

```python
import functools

import jax
import jax.numpy as jnp
from jax import lax
from jax.experimental import pallas as pl
from jax.experimental.pallas import tpu as pltpu
from jax.sharding import PartitionSpec as P

F32 = jnp.float32
BF16 = jnp.bfloat16
MESH = pl.DeviceIdType.MESH
ROWS = (((1,), (1,)), ((), ()))
COLS = (((0,), (0,)), ((), ()))


def place(axis):
    size = lax.axis_size(axis)
    me = lax.axis_index(axis)
    return me, me // 2, lax.rem(me, 2), size // 2


def remote(src, dst, send, recv, axis, index):
    return pltpu.make_async_remote_copy(
        src_ref=src,
        dst_ref=dst,
        send_sem=send,
        recv_sem=recv,
        device_id={axis: index},
        device_id_type=MESH,
    )


def greet(pairs_axes, all_axes):
    barrier = pltpu.get_barrier_semaphore()
    count = 0
    for axis in pairs_axes:
        me, half, side, halves = place(axis)
        targets = [half * 2 + 1 - side]
        targets += [lax.rem(half + j, halves) * 2 + side for j in range(1, halves)]
        for index in targets:
            pl.semaphore_signal(barrier, inc=1, device_id={axis: index}, device_id_type=MESH)
        count += len(targets)
    for axis in all_axes:
        me, size = lax.axis_index(axis), lax.axis_size(axis)
        for j in range(1, size):
            pl.semaphore_signal(
                barrier, inc=1, device_id={axis: lax.rem(me + j, size)}, device_id_type=MESH
            )
        count += size - 1
    pl.semaphore_wait(barrier, count)


def swap_starts(ins, outs, send, recv):
    me, size = lax.axis_index("expert"), lax.axis_size("expert")
    started = []
    for j in range(1, size):
        for i, (src, dst) in enumerate(zip(ins, outs)):
            other = lax.rem(me + j, size)
            copy = remote(
                src.at[other], dst.at[me], send.at[i, j - 1], recv.at[i, j - 1], "expert", other
            )
            copy.start()
            started.append(copy)
    return started


def dispatch_kernel(gathered, swapped, *refs):
    ag_in, refs = refs[:gathered], refs[gathered:]
    sw_in, refs = refs[:swapped], refs[swapped:]
    ag_out, refs = refs[:gathered], refs[gathered:]
    sw_out, refs = refs[:swapped], refs[swapped:]
    ag_own, refs = refs[:gathered], refs[gathered:]
    sw_own, refs = refs[:swapped], refs[swapped:]
    own_sem, side_send, side_recv, far_send, far_recv, fwd_send, fwd_recv, sw_send, sw_recv = refs
    me, half, side, halves = place("dp")
    rank = lax.axis_index("expert")
    partner = half * 2 + 1 - side
    greet(("dp",), ("expert",))
    far = {}
    for i in range(gathered):
        for j in range(1, halves):
            other = lax.rem(half + j, halves) * 2 + side
            far[i, j] = remote(
                ag_in[i], ag_out[i].at[me], far_send.at[i, j - 1], far_recv.at[i, j - 1], "dp", other
            )
            far[i, j].start()
    swaps = swap_starts(sw_in, sw_out, sw_send, sw_recv)
    sides = []
    for i in range(gathered):
        copy = remote(ag_in[i], ag_out[i].at[me], side_send.at[i], side_recv.at[i], "dp", partner)
        copy.start()
        sides.append(copy)
    loads = []
    for i in range(gathered):
        loads.append((ag_in[i], ag_own[i], ag_out[i].at[me]))
    for i in range(swapped):
        loads.append((sw_in[i].at[rank], sw_own[i], sw_out[i].at[rank]))
    for i, (src, mid, _) in enumerate(loads):
        pltpu.make_async_copy(src, mid, own_sem.at[i]).start()
    for i, (src, mid, dst) in enumerate(loads):
        pltpu.make_async_copy(src, mid, own_sem.at[i]).wait()
        pltpu.make_async_copy(mid, dst, own_sem.at[i]).start()
    forwards = []
    for i in range(gathered):
        for j in range(1, halves):
            far[i, j].wait_recv()
            origin = lax.rem(half + halves - j, halves) * 2 + side
            block = ag_out[i].at[origin]
            copy = remote(
                block, block, fwd_send.at[i, j - 1], fwd_recv.at[i, j - 1], "dp", partner
            )
            copy.start()
            forwards.append(copy)
    for i, (src, mid, dst) in enumerate(loads):
        pltpu.make_async_copy(mid, dst, own_sem.at[i]).wait()
    for copy in far.values():
        copy.wait_send()
    for copy in sides + swaps + forwards:
        copy.wait()


def dispatch(gather, swap):
    ways = lax.axis_size("dp")
    size = lax.axis_size("expert")
    halves = ways // 2
    ng, ns = len(gather), len(swap)
    dma = pltpu.SemaphoreType.DMA
    anywhere = pl.BlockSpec(memory_space=pl.ANY)
    shapes = [jax.ShapeDtypeStruct((ways,) + a.shape, a.dtype) for a in gather]
    shapes += [jax.ShapeDtypeStruct(a.shape, a.dtype) for a in swap]
    outs = pl.pallas_call(
        functools.partial(dispatch_kernel, ng, ns),
        out_shape=shapes,
        in_specs=[anywhere] * (ng + ns),
        out_specs=[anywhere] * (ng + ns),
        scratch_shapes=[pltpu.VMEM(a.shape, a.dtype) for a in gather]
        + [pltpu.VMEM(a.shape[1:], a.dtype) for a in swap]
        + [
            dma((ng + ns,)),
            dma((ng,)),
            dma((ng,)),
            dma((ng, halves - 1)),
            dma((ng, halves - 1)),
            dma((ng, halves - 1)),
            dma((ng, halves - 1)),
            dma((ns, size - 1)),
            dma((ns, size - 1)),
        ],
        compiler_params=pltpu.CompilerParams(
            collective_id=0, has_side_effects=True, vmem_limit_bytes=20 << 20
        ),
        name="dispatch",
    )(*gather, *swap)
    return outs[:ng], outs[ng:]


def add_rows(dst, srcs):
    rows = dst.shape[0]
    step = 16 if rows % 16 == 0 else rows

    def body(i, carry):
        at = pl.ds(pl.multiple_of(i * step, step), step)
        total = srcs[0][at, :].astype(F32)
        for src in srcs[1:]:
            total = total + src[at, :].astype(F32)
        dst[at, :] = total.astype(dst.dtype)
        return carry

    lax.fori_loop(0, rows // step, body, 0)


def combine_kernel(axes, swapped, *refs):
    count = len(axes)
    rs_in, refs = refs[:count], refs[count:]
    sw_in, refs = refs[:swapped], refs[swapped:]
    rs_out, refs = refs[:count], refs[count:]
    sw_out, refs = refs[:swapped], refs[swapped:]
    sw_own, refs = refs[:swapped], refs[swapped:]
    own_sem, sw_send, sw_recv = refs[:3]
    bufs = [refs[3 + 11 * i : 14 + 11 * i] for i in range(count)]
    rank = lax.axis_index("expert")
    greet(("dp",), ("expert",))
    sides, mines = {}, {}
    deepest = max(lax.axis_size(axis) // 2 for axis in axes)
    for turn in range(1, deepest + 1):
        for i, axis in enumerate(axes):
            _, half, side, halves = place(axis)
            if turn > halves:
                continue
            j = turn % halves
            arrived, held, _, _, _, load_sem, s_send, s_recv = bufs[i][:8]
            to = lax.rem(half + j, halves) * 2
            partner = half * 2 + 1 - side
            sides[i, j] = remote(
                rs_in[i].at[to + 1 - side], arrived.at[j], s_send.at[j], s_recv.at[j], axis, partner
            )
            sides[i, j].start()
            mines[i, j] = pltpu.make_async_copy(
                rs_in[i].at[to + side], held.at[j], load_sem.at[j]
            )
            mines[i, j].start()
    swaps = swap_starts(sw_in, sw_out, sw_send, sw_recv)
    for i in range(swapped):
        pltpu.make_async_copy(sw_in[i].at[rank], sw_own[i], own_sem.at[i]).start()
    for i in range(swapped):
        pltpu.make_async_copy(sw_in[i].at[rank], sw_own[i], own_sem.at[i]).wait()
        pltpu.make_async_copy(sw_own[i], sw_out[i].at[rank], own_sem.at[i]).start()
    fars = {}
    for i, axis in enumerate(axes):
        _, half, side, halves = place(axis)
        arrived, held, summed, landed, _, _, _, _, f_send, f_recv, _ = bufs[i]
        for j in range(1, halves):
            sides[i, j].wait_recv()
            mines[i, j].wait()
            add_rows(summed.at[j - 1], [arrived.at[j], held.at[j]])
            other = lax.rem(half + j, halves) * 2 + side
            fars[i, j] = remote(
                summed.at[j - 1], landed.at[j - 1], f_send.at[j - 1], f_recv.at[j - 1], axis, other
            )
            fars[i, j].start()
    puts = []
    for i, axis in enumerate(axes):
        halves = lax.axis_size(axis) // 2
        arrived, held, summed, landed, result, _, _, _, _, _, out_sem = bufs[i]
        sides[i, 0].wait_recv()
        mines[i, 0].wait()
        for j in range(1, halves):
            fars[i, j].wait_recv()
        add_rows(
            result, [arrived.at[0], held.at[0]] + [landed.at[j - 1] for j in range(1, halves)]
        )
        put = pltpu.make_async_copy(result, rs_out[i], out_sem.at[0])
        put.start()
        puts.append(put)
    for i in range(swapped):
        pltpu.make_async_copy(sw_own[i], sw_out[i].at[rank], own_sem.at[i]).wait()
    for copy in list(sides.values()) + list(fars.values()):
        copy.wait_send()
    for copy in swaps + puts:
        copy.wait()


def combine(reduce, swap):
    size = lax.axis_size("expert")
    nr, ns = len(reduce), len(swap)
    dma = pltpu.SemaphoreType.DMA
    anywhere = pl.BlockSpec(memory_space=pl.ANY)
    shapes = [jax.ShapeDtypeStruct(a.shape[1:], kind) for _, a, kind in reduce]
    shapes += [jax.ShapeDtypeStruct(a.shape, a.dtype) for a in swap]
    scratch = [pltpu.VMEM(a.shape[1:], a.dtype) for a in swap]
    scratch += [dma((ns,)), dma((ns, size - 1)), dma((ns, size - 1))]
    for axis, a, kind in reduce:
        halves = lax.axis_size(axis) // 2
        block = a.shape[1:]
        scratch += [
            pltpu.VMEM((halves,) + block, a.dtype),
            pltpu.VMEM((halves,) + block, a.dtype),
            pltpu.VMEM((halves - 1,) + block, a.dtype),
            pltpu.VMEM((halves - 1,) + block, a.dtype),
            pltpu.VMEM(block, kind),
            dma((halves,)),
            dma((halves,)),
            dma((halves,)),
            dma((halves - 1,)),
            dma((halves - 1,)),
            dma((1,)),
        ]
    outs = pl.pallas_call(
        functools.partial(combine_kernel, tuple(axis for axis, _, _ in reduce), ns),
        out_shape=shapes,
        in_specs=[anywhere] * (nr + ns),
        out_specs=[anywhere] * (nr + ns),
        scratch_shapes=scratch,
        compiler_params=pltpu.CompilerParams(
            collective_id=1, has_side_effects=True, vmem_limit_bytes=56 << 20
        ),
        name="combine",
    )(*[a for _, a, _ in reduce], *swap)
    return outs[:nr], outs[nr:]


def dot(a, b, dims=None):
    if dims is None:
        return jnp.dot(a, b, preferred_element_type=F32)
    return lax.dot_general(a, b, dims, preferred_element_type=F32)


def expert_block(rows_x, rows_d, w_gate, w_up, w_down):
    pre_gate = dot(rows_x, w_gate, ROWS)
    pre_up = dot(rows_x, w_up, ROWS)
    sigma = jax.nn.sigmoid(pre_gate)
    act = (pre_gate * sigma * pre_up).astype(BF16)
    out = dot(act, w_down).astype(BF16)
    d_act = dot(rows_d, w_down, ROWS)
    slope = sigma * (1.0 + pre_gate * (1.0 - sigma))
    d_gate = (d_act * pre_up * slope).astype(BF16)
    d_up = (d_act * pre_gate * sigma).astype(BF16)
    dx = (dot(d_gate, w_gate) + dot(d_up, w_up)).astype(BF16)
    return (
        out,
        dx,
        dot(d_gate, rows_x, COLS).astype(BF16),
        dot(d_up, rows_x, COLS).astype(BF16),
        dot(act, rows_d, COLS).astype(BF16),
    )


def local(
    tokens,
    cotangent,
    route_ids,
    route_weights,
    cold_gate,
    cold_up,
    cold_down,
    hot_gate,
    hot_up,
    hot_down,
):
    tok_rows, width = tokens.shape
    top_count = route_ids.shape[1]
    owners = lax.axis_size("expert")
    replicas = lax.axis_size("dp")
    hot_count, hot_units = hot_gate.shape[:2]
    hot_load = tok_rows // 4
    cold_slots = tok_rows * top_count - hot_count * hot_load
    capacity = max(2, 5 * cold_slots // (4 * owners) + 1)
    capacity = (capacity + 7) // 8 * 8
    cold_total = owners * capacity
    hot_rows = hot_count * hot_load
    slot_total = cold_total + hot_rows

    ids_row = route_ids.T
    earlier = lax.broadcasted_iota(jnp.int32, (tok_rows, tok_rows), 0) < lax.broadcasted_iota(
        jnp.int32, (tok_rows, tok_rows), 1
    )
    slots = lax.broadcasted_iota(jnp.int32, (slot_total, tok_rows), 0)
    placing, pieces = [], []
    for k in range(top_count):
        mine = ids_row[k][None, :]
        same = sum((route_ids[:, o][:, None] == mine).astype(jnp.int32) for o in range(top_count))
        rank = jnp.sum(jnp.where(earlier, same, 0), axis=0)[None, :]
        target = jnp.where(
            mine < owners,
            mine * capacity + rank,
            cold_total + (mine - owners) * hot_load + rank,
        )
        hit = slots == target
        placing.append(hit.astype(BF16))
        pieces.append(jnp.where(hit, route_weights[:, k][None, :], 0.0))
    either = sum(placing[1:], placing[0])
    gain = jnp.sum(sum(pieces[1:], pieces[0]), axis=1, keepdims=True)
    send_x = dot(either, tokens).astype(BF16)
    send_d = (gain * dot(either, cotangent)).astype(BF16)

    (g_gate, g_up, g_down, hot_x, hot_d), (cold_x, cold_d) = dispatch(
        (cold_gate[0], cold_up[0], cold_down[0], send_x[cold_total:], send_d[cold_total:]),
        (
            send_x[:cold_total].reshape(owners, capacity, width),
            send_d[:cold_total].reshape(owners, capacity, width),
        ),
    )

    hot_outs, hot_dxs, hot_grads = [], [], []
    for h in range(hot_count):
        rows_x = hot_x[:, h * hot_load : (h + 1) * hot_load].reshape(-1, width)
        rows_d = hot_d[:, h * hot_load : (h + 1) * hot_load].reshape(-1, width)
        out, dx, *grads = expert_block(rows_x, rows_d, hot_gate[h], hot_up[h], hot_down[h])
        hot_outs.append(out.reshape(replicas, hot_load, width))
        hot_dxs.append(dx.reshape(replicas, hot_load, width))
        hot_grads.append(grads)
    hot_out = jnp.concatenate(hot_outs, axis=1)
    hot_dx = jnp.concatenate(hot_dxs, axis=1)
    blocks = [
        jnp.concatenate([grads[m] for grads in hot_grads], axis=0)
        .reshape(hot_count * hot_units, owners, width // owners)
        .transpose(1, 0, 2)
        for m in range(3)
    ]

    out, dx, *terms = expert_block(
        cold_x.reshape(cold_total, width),
        cold_d.reshape(cold_total, width),
        g_gate.reshape(-1, width),
        g_up.reshape(-1, width),
        g_down.reshape(-1, width),
    )
    units = cold_gate.shape[1]
    terms = [term.reshape(replicas, units, width) for term in terms]
    sums, (back_out, back_dx) = combine(
        [("dp", term, BF16) for term in terms]
        + [("dp", hot_out, BF16), ("dp", hot_dx, BF16)]
        + [("expert", block, F32) for block in blocks],
        (out.reshape(owners, capacity, width), dx.reshape(owners, capacity, width)),
    )
    back_outs = jnp.concatenate([back_out.reshape(cold_total, width), sums[3]], axis=0)
    back_grads = jnp.concatenate([back_dx.reshape(cold_total, width), sums[4]], axis=0)
    outs = [dot(p, back_outs, COLS) for p in placing]
    mixed = sum(route_weights[:, k][:, None] * outs[k] for k in range(top_count)).astype(BF16)
    cot = cotangent.astype(F32)
    route_grad = jnp.stack([jnp.sum(cot * o, axis=1) for o in outs], axis=1)
    token_grad = dot(either, back_grads, COLS).astype(BF16)
    hot_sums = [s.reshape(hot_count, hot_units, width // owners) for s in sums[5:]]
    return (mixed, token_grad, route_grad, sums[0][None], sums[1][None], sums[2][None], *hot_sums)


def solution(mesh):
    rows = P(("expert", "dp"), None)
    owned = P("expert", "dp", None)
    hot = P(None, "dp", None)
    hot_out = P(None, "dp", "expert")
    return jax.shard_map(
        local,
        mesh=mesh,
        in_specs=(rows,) * 4 + (owned,) * 3 + (hot,) * 3,
        out_specs=(rows,) * 3 + (owned,) * 3 + (hot_out,) * 3,
        check_vma=False,
    )
```

```python
import functools

import jax
import jax.numpy as jnp
from jax import lax
from jax.experimental import pallas as pl
from jax.experimental.pallas import tpu as pltpu
from jax.sharding import PartitionSpec as P

F32 = jnp.float32
BF16 = jnp.bfloat16
MESH = pl.DeviceIdType.MESH
ROWS = (((1,), (1,)), ((), ()))
COLS = (((0,), (0,)), ((), ()))


def place(axis):
    size = lax.axis_size(axis)
    me = lax.axis_index(axis)
    return me, me // 2, lax.rem(me, 2), size // 2


def remote(src, dst, send, recv, axis, index):
    return pltpu.make_async_remote_copy(
        src_ref=src,
        dst_ref=dst,
        send_sem=send,
        recv_sem=recv,
        device_id={axis: index},
        device_id_type=MESH,
    )


def greet(pairs_axes, all_axes):
    barrier = pltpu.get_barrier_semaphore()
    count = 0
    for axis in pairs_axes:
        me, half, side, halves = place(axis)
        targets = [half * 2 + 1 - side]
        targets += [lax.rem(half + j, halves) * 2 + side for j in range(1, halves)]
        for index in targets:
            pl.semaphore_signal(barrier, inc=1, device_id={axis: index}, device_id_type=MESH)
        count += len(targets)
    for axis in all_axes:
        me, size = lax.axis_index(axis), lax.axis_size(axis)
        for j in range(1, size):
            pl.semaphore_signal(
                barrier, inc=1, device_id={axis: lax.rem(me + j, size)}, device_id_type=MESH
            )
        count += size - 1
    pl.semaphore_wait(barrier, count)


def swap_starts(ins, outs, send, recv):
    me, size = lax.axis_index("expert"), lax.axis_size("expert")
    started = []
    for j in range(1, size):
        for i, (src, dst) in enumerate(zip(ins, outs)):
            other = lax.rem(me + j, size)
            copy = remote(
                src.at[other], dst.at[me], send.at[i, j - 1], recv.at[i, j - 1], "expert", other
            )
            copy.start()
            started.append(copy)
    return started


def dispatch_kernel(gathered, swapped, *refs):
    ag_in, refs = refs[:gathered], refs[gathered:]
    sw_in, refs = refs[:swapped], refs[swapped:]
    ag_out, refs = refs[:gathered], refs[gathered:]
    sw_out, refs = refs[:swapped], refs[swapped:]
    ag_own, refs = refs[:gathered], refs[gathered:]
    sw_own, refs = refs[:swapped], refs[swapped:]
    own_sem, side_send, side_recv, far_send, far_recv, fwd_send, fwd_recv, sw_send, sw_recv = refs
    me, half, side, halves = place("dp")
    rank = lax.axis_index("expert")
    partner = half * 2 + 1 - side
    greet(("dp",), ("expert",))
    far = {}
    for i in range(gathered):
        for j in range(1, halves):
            other = lax.rem(half + j, halves) * 2 + side
            far[i, j] = remote(
                ag_in[i], ag_out[i].at[me], far_send.at[i, j - 1], far_recv.at[i, j - 1], "dp", other
            )
            far[i, j].start()
    swaps = swap_starts(sw_in, sw_out, sw_send, sw_recv)
    sides = []
    for i in range(gathered):
        copy = remote(ag_in[i], ag_out[i].at[me], side_send.at[i], side_recv.at[i], "dp", partner)
        copy.start()
        sides.append(copy)
    loads = []
    for i in range(gathered):
        loads.append((ag_in[i], ag_own[i], ag_out[i].at[me]))
    for i in range(swapped):
        loads.append((sw_in[i].at[rank], sw_own[i], sw_out[i].at[rank]))
    for i, (src, mid, _) in enumerate(loads):
        pltpu.make_async_copy(src, mid, own_sem.at[i]).start()
    for i, (src, mid, dst) in enumerate(loads):
        pltpu.make_async_copy(src, mid, own_sem.at[i]).wait()
        pltpu.make_async_copy(mid, dst, own_sem.at[i]).start()
    forwards = []
    for i in range(gathered):
        for j in range(1, halves):
            far[i, j].wait_recv()
            origin = lax.rem(half + halves - j, halves) * 2 + side
            block = ag_out[i].at[origin]
            copy = remote(
                block, block, fwd_send.at[i, j - 1], fwd_recv.at[i, j - 1], "dp", partner
            )
            copy.start()
            forwards.append(copy)
    for i, (src, mid, dst) in enumerate(loads):
        pltpu.make_async_copy(mid, dst, own_sem.at[i]).wait()
    for copy in far.values():
        copy.wait_send()
    for copy in sides + swaps + forwards:
        copy.wait()


def dispatch(gather, swap):
    ways = lax.axis_size("dp")
    size = lax.axis_size("expert")
    halves = ways // 2
    ng, ns = len(gather), len(swap)
    dma = pltpu.SemaphoreType.DMA
    anywhere = pl.BlockSpec(memory_space=pl.ANY)
    shapes = [jax.ShapeDtypeStruct((ways,) + a.shape, a.dtype) for a in gather]
    shapes += [jax.ShapeDtypeStruct(a.shape, a.dtype) for a in swap]
    outs = pl.pallas_call(
        functools.partial(dispatch_kernel, ng, ns),
        out_shape=shapes,
        in_specs=[anywhere] * (ng + ns),
        out_specs=[anywhere] * (ng + ns),
        scratch_shapes=[pltpu.VMEM(a.shape, a.dtype) for a in gather]
        + [pltpu.VMEM(a.shape[1:], a.dtype) for a in swap]
        + [
            dma((ng + ns,)),
            dma((ng,)),
            dma((ng,)),
            dma((ng, halves - 1)),
            dma((ng, halves - 1)),
            dma((ng, halves - 1)),
            dma((ng, halves - 1)),
            dma((ns, size - 1)),
            dma((ns, size - 1)),
        ],
        compiler_params=pltpu.CompilerParams(
            collective_id=0, has_side_effects=True, vmem_limit_bytes=20 << 20
        ),
        name="dispatch",
    )(*gather, *swap)
    return outs[:ng], outs[ng:]


def add_rows(dst, srcs):
    rows = dst.shape[0]
    step = 16 if rows % 16 == 0 else rows

    def body(i, carry):
        at = pl.ds(pl.multiple_of(i * step, step), step)
        total = srcs[0][at, :].astype(F32)
        for src in srcs[1:]:
            total = total + src[at, :].astype(F32)
        dst[at, :] = total.astype(dst.dtype)
        return carry

    lax.fori_loop(0, rows // step, body, 0)


def combine_kernel(axes, swapped, *refs):
    count = len(axes)
    rs_in, refs = refs[:count], refs[count:]
    sw_in, refs = refs[:swapped], refs[swapped:]
    rs_out, refs = refs[:count], refs[count:]
    sw_out, refs = refs[:swapped], refs[swapped:]
    sw_own, refs = refs[:swapped], refs[swapped:]
    own_sem, sw_send, sw_recv = refs[:3]
    bufs = [refs[3 + 11 * i : 14 + 11 * i] for i in range(count)]
    rank = lax.axis_index("expert")
    greet(("dp",), ("expert",))
    sides, mines = {}, {}
    deepest = max(lax.axis_size(axis) // 2 for axis in axes)
    for turn in range(1, deepest + 1):
        for i, axis in enumerate(axes):
            _, half, side, halves = place(axis)
            if turn > halves:
                continue
            j = turn % halves
            arrived, held, _, _, _, load_sem, s_send, s_recv = bufs[i][:8]
            to = lax.rem(half + j, halves) * 2
            partner = half * 2 + 1 - side
            sides[i, j] = remote(
                rs_in[i].at[to + 1 - side], arrived.at[j], s_send.at[j], s_recv.at[j], axis, partner
            )
            sides[i, j].start()
            mines[i, j] = pltpu.make_async_copy(
                rs_in[i].at[to + side], held.at[j], load_sem.at[j]
            )
            mines[i, j].start()
    swaps = swap_starts(sw_in, sw_out, sw_send, sw_recv)
    for i in range(swapped):
        pltpu.make_async_copy(sw_in[i].at[rank], sw_own[i], own_sem.at[i]).start()
    for i in range(swapped):
        pltpu.make_async_copy(sw_in[i].at[rank], sw_own[i], own_sem.at[i]).wait()
        pltpu.make_async_copy(sw_own[i], sw_out[i].at[rank], own_sem.at[i]).start()
    fars = {}
    for i, axis in enumerate(axes):
        _, half, side, halves = place(axis)
        arrived, held, summed, landed, _, _, _, _, f_send, f_recv, _ = bufs[i]
        for j in range(1, halves):
            sides[i, j].wait_recv()
            mines[i, j].wait()
            add_rows(summed.at[j - 1], [arrived.at[j], held.at[j]])
            other = lax.rem(half + j, halves) * 2 + side
            fars[i, j] = remote(
                summed.at[j - 1], landed.at[j - 1], f_send.at[j - 1], f_recv.at[j - 1], axis, other
            )
            fars[i, j].start()
    puts = []
    for i, axis in enumerate(axes):
        halves = lax.axis_size(axis) // 2
        arrived, held, summed, landed, result, _, _, _, _, _, out_sem = bufs[i]
        sides[i, 0].wait_recv()
        mines[i, 0].wait()
        for j in range(1, halves):
            fars[i, j].wait_recv()
        add_rows(
            result, [arrived.at[0], held.at[0]] + [landed.at[j - 1] for j in range(1, halves)]
        )
        put = pltpu.make_async_copy(result, rs_out[i], out_sem.at[0])
        put.start()
        puts.append(put)
    for i in range(swapped):
        pltpu.make_async_copy(sw_own[i], sw_out[i].at[rank], own_sem.at[i]).wait()
    for copy in list(sides.values()) + list(fars.values()):
        copy.wait_send()
    for copy in swaps + puts:
        copy.wait()


def combine(reduce, swap):
    size = lax.axis_size("expert")
    nr, ns = len(reduce), len(swap)
    dma = pltpu.SemaphoreType.DMA
    anywhere = pl.BlockSpec(memory_space=pl.ANY)
    shapes = [jax.ShapeDtypeStruct(a.shape[1:], kind) for _, a, kind in reduce]
    shapes += [jax.ShapeDtypeStruct(a.shape, a.dtype) for a in swap]
    scratch = [pltpu.VMEM(a.shape[1:], a.dtype) for a in swap]
    scratch += [dma((ns,)), dma((ns, size - 1)), dma((ns, size - 1))]
    for axis, a, kind in reduce:
        halves = lax.axis_size(axis) // 2
        block = a.shape[1:]
        scratch += [
            pltpu.VMEM((halves,) + block, a.dtype),
            pltpu.VMEM((halves,) + block, a.dtype),
            pltpu.VMEM((halves - 1,) + block, a.dtype),
            pltpu.VMEM((halves - 1,) + block, a.dtype),
            pltpu.VMEM(block, kind),
            dma((halves,)),
            dma((halves,)),
            dma((halves,)),
            dma((halves - 1,)),
            dma((halves - 1,)),
            dma((1,)),
        ]
    outs = pl.pallas_call(
        functools.partial(combine_kernel, tuple(axis for axis, _, _ in reduce), ns),
        out_shape=shapes,
        in_specs=[anywhere] * (nr + ns),
        out_specs=[anywhere] * (nr + ns),
        scratch_shapes=scratch,
        compiler_params=pltpu.CompilerParams(
            collective_id=1, has_side_effects=True, vmem_limit_bytes=56 << 20
        ),
        name="combine",
    )(*[a for _, a, _ in reduce], *swap)
    return outs[:nr], outs[nr:]


def dot(a, b, dims=None):
    if dims is None:
        return jnp.dot(a, b, preferred_element_type=F32)
    return lax.dot_general(a, b, dims, preferred_element_type=F32)


def expert_block(rows_x, rows_d, w_gate, w_up, w_down):
    pre_gate = dot(rows_x, w_gate, ROWS)
    pre_up = dot(rows_x, w_up, ROWS)
    sigma = jax.nn.sigmoid(pre_gate)
    act = (pre_gate * sigma * pre_up).astype(BF16)
    out = dot(act, w_down).astype(BF16)
    d_act = dot(rows_d, w_down, ROWS)
    slope = sigma * (1.0 + pre_gate * (1.0 - sigma))
    d_gate = (d_act * pre_up * slope).astype(BF16)
    d_up = (d_act * pre_gate * sigma).astype(BF16)
    dx = (dot(d_gate, w_gate) + dot(d_up, w_up)).astype(BF16)
    return (
        out,
        dx,
        dot(d_gate, rows_x, COLS).astype(BF16),
        dot(d_up, rows_x, COLS).astype(BF16),
        dot(act, rows_d, COLS).astype(BF16),
    )


def mix(pre_gate, pre_up):
    sigma = 1.0 / (1.0 + jnp.exp(-pre_gate))
    return sigma, pre_gate * sigma


def layer_kernel(*refs):
    hot_in, cold_in, own_w, hot_w = refs[:2], refs[2:4], refs[4:7], refs[7:10]
    back, sums, hot_sums, hot_grads = refs[10:12], refs[12:15], refs[15:17], refs[17:20]
    hot_rows, weights, landing, packed = refs[20:22], refs[22:25], refs[25:27], refs[27:29]
    pre_g, pre_u, act, d_gate, d_up = refs[29:34]
    results, terms, hot_parts, hot_terms = refs[34:36], refs[36:39], refs[39:41], refs[41:44]
    arrived, summed, landed = refs[44:49], refs[49:54], refs[54:59]
    e_arrived, e_held, e_summed, e_landed = refs[59:62], refs[62:65], refs[65:68], refs[68:71]
    (own_sem, ag_fs, ag_fr, ag_ss, ag_sr, ag_ws, ag_wr, sw_s, sw_r, bk_s, bk_r) = refs[71:82]
    (rs_ss, rs_sr, rs_fs, rs_fr, ex_ss, ex_sr, ex_fs, ex_fr, ex_l) = refs[82:91]
    me, half, side, halves = place("dp")
    rank, e_half, e_side, e_halves = place("expert")
    owners = 2 * e_halves
    partner, e_partner = half * 2 + 1 - side, e_half * 2 + 1 - e_side
    slots = 2 * halves
    load, width = hot_in[0].shape
    cap = cold_in[0].shape[1]
    part = width // owners
    tile = 512 if width % 512 == 0 else width
    pending = []

    def go(copy):
        copy.start()
        return copy

    def slot_of(buffer, s):
        if len(buffer.shape) == 2:
            return buffer.at[pl.ds(s * load, load)]
        return buffer.at[s]

    def tiles(body):
        def step(i, carry):
            body(pl.ds(pl.multiple_of(i * tile, tile), tile))
            return carry

        lax.fori_loop(0, width // tile, step, 0)

    greet(("dp",), ("expert",))
    sources = list(hot_in) + list(own_w)
    targets = list(hot_rows) + list(weights)
    far, near, forwarded, own = {}, {}, {}, {}

    def send_near(i):
        near[i] = go(
            remote(sources[i], slot_of(targets[i], 1), ag_ss.at[i], ag_sr.at[i], "dp", partner)
        )
        own[i] = go(pltpu.make_async_copy(sources[i], slot_of(targets[i], 0), own_sem.at[i]))

    def forward(i):
        for j in range(1, halves):
            far[i, j].wait_recv()
            forwarded[i, j] = go(
                remote(
                    slot_of(targets[i], 2 * j),
                    slot_of(targets[i], 2 * j + 1),
                    ag_ws.at[i, j - 1],
                    ag_wr.at[i, j - 1],
                    "dp",
                    partner,
                )
            )

    for i in range(5):
        for j in range(1, halves):
            other = lax.rem(half + j, halves) * 2 + side
            far[i, j] = go(
                remote(
                    sources[i],
                    slot_of(targets[i], 2 * j),
                    ag_fs.at[i, j - 1],
                    ag_fr.at[i, j - 1],
                    "dp",
                    other,
                )
            )
    swaps, mine = [], []
    for i in range(2):
        for j in range(1, owners):
            other = lax.rem(rank + j, owners)
            swaps.append(
                go(
                    remote(
                        cold_in[i].at[other],
                        landing[i].at[rank],
                        sw_s.at[i, j - 1],
                        sw_r.at[i, j - 1],
                        "expert",
                        other,
                    )
                )
            )
        mine.append(
            go(
                pltpu.make_async_copy(
                    cold_in[i].at[rank], landing[i].at[rank], own_sem.at[5 + i]
                )
            )
        )
    for i in range(5):
        send_near(i)

    for i in (0, 1):
        forward(i)
    for i in (0, 1):
        near[i].wait_recv()
        own[i].wait()
        for j in range(1, halves):
            forwarded[i, j].wait_recv()
    w_gate, w_up, w_down = hot_w
    gate = dot(hot_rows[0][...], w_gate[...], ROWS)
    up = dot(hot_rows[0][...], w_up[...], ROWS)
    sigma, silu = mix(gate, up)
    d_act = dot(hot_rows[1][...], w_down[...], ROWS)
    h_act = (silu * up).astype(BF16)
    h_dg = (d_act * up * (sigma * (1.0 + gate * (1.0 - sigma)))).astype(BF16)
    h_du = (d_act * silu).astype(BF16)

    def hot_tile(at):
        hot_parts[0][:, at] = dot(h_act, w_down[:, at]).astype(BF16)
        hot_parts[1][:, at] = (dot(h_dg, w_gate[:, at]) + dot(h_du, w_up[:, at])).astype(BF16)
        hot_terms[0][:, at] = dot(h_dg, hot_rows[0][:, at], COLS).astype(BF16)
        hot_terms[1][:, at] = dot(h_du, hot_rows[0][:, at], COLS).astype(BF16)
        hot_terms[2][:, at] = dot(h_act, hot_rows[1][:, at], COLS).astype(BF16)

    tiles(hot_tile)

    locals_ = list(terms) + list(hot_parts)
    rs_near, rs_far, ex_near, ex_far, ex_held = {}, {}, {}, {}, {}

    def reduce_near(i, j):
        rs_near[i, j] = go(
            remote(
                slot_of(locals_[i], 2 * j + 1),
                arrived[i].at[j],
                rs_ss.at[i, j],
                rs_sr.at[i, j],
                "dp",
                partner,
            )
        )

    def reduce_far(i, j):
        rs_near[i, j].wait_recv()
        add_rows(summed[i].at[j - 1], [arrived[i].at[j], slot_of(locals_[i], 2 * j)])
        other = lax.rem(half + halves - j, halves) * 2 + side
        rs_far[i, j] = go(
            remote(
                summed[i].at[j - 1],
                landed[i].at[j - 1],
                rs_fs.at[i, j - 1],
                rs_fr.at[i, j - 1],
                "dp",
                other,
            )
        )

    def columns(index):
        return pl.ds(pl.multiple_of(index * part, 128), part)

    for i in range(3):
        for j in list(range(1, e_halves)) + [0]:
            to = lax.rem(e_half + j, e_halves) * 2
            ex_near[i, j] = go(
                remote(
                    hot_terms[i].at[:, columns(to + 1 - e_side)],
                    e_arrived[i].at[j],
                    ex_ss.at[i, j],
                    ex_sr.at[i, j],
                    "expert",
                    e_partner,
                )
            )
            ex_held[i, j] = go(
                pltpu.make_async_copy(
                    hot_terms[i].at[:, columns(to + e_side)], e_held[i].at[j], ex_l.at[i, j]
                )
            )
    for i in (3, 4):
        for j in range(halves - 1, -1, -1):
            reduce_near(i, j)

    def repack(i):
        def step(k, carry):
            a, b = landing[i][2 * k].astype(F32), landing[i][2 * k + 1].astype(F32)
            at = pl.ds(pl.multiple_of(k * 2 * cap, 16), 2 * cap)
            packed[i][at, :] = jnp.concatenate([a, b], axis=0).astype(BF16)
            return carry

        lax.fori_loop(0, owners // 2, step, 0)

    def give_back(i):
        for j in range(1, owners):
            other = lax.rem(rank + j, owners)
            pending.append(
                go(
                    remote(
                        results[i].at[other],
                        back[i].at[rank],
                        bk_s.at[i, j - 1],
                        bk_r.at[i, j - 1],
                        "expert",
                        other,
                    )
                )
            )
        pending.append(
            go(pltpu.make_async_copy(results[i].at[rank], back[i].at[rank], own_sem.at[7 + i]))
        )

    def put_rows(i, at, value):
        for e in range(owners):
            results[i][e, :, at] = value[e * cap : (e + 1) * cap].astype(BF16)

    for copy in swaps[: owners - 1]:
        copy.wait_recv()
    mine[0].wait()
    repack(0)
    for i in (2, 3, 4):
        near[i].wait_recv()
        own[i].wait()

    def project(m, dst, first, last):
        def step(s, carry):
            dst[s] = dot(packed[0][...], weights[m][s], ROWS)
            return carry

        lax.fori_loop(first, last, step, 0)

    project(0, pre_g, 0, 2)
    project(1, pre_u, 0, 2)
    forward(2)
    for j in range(1, halves):
        forwarded[2, j].wait_recv()
    project(0, pre_g, 2, slots)
    forward(3)
    for j in range(1, halves):
        forwarded[3, j].wait_recv()
    project(1, pre_u, 2, slots)

    def activate(s, carry):
        _, silu = mix(pre_g[s], pre_u[s])
        act[s] = (silu * pre_u[s]).astype(BF16)
        return carry

    lax.fori_loop(0, slots, activate, 0)
    forward(4)
    for j in range(1, halves):
        forwarded[4, j].wait_recv()

    def out_tile(at):
        total = dot(act[0], weights[2][0, :, at])
        for s in range(1, slots):
            total = total + dot(act[s], weights[2][s, :, at])
        put_rows(0, at, total)

    tiles(out_tile)

    for copy in swaps[owners - 1 :]:
        copy.wait_recv()
    mine[1].wait()
    give_back(0)
    repack(1)

    def slope(s, carry):
        d_act = dot(packed[1][...], weights[2][s], ROWS)
        gate, up = pre_g[s], pre_u[s]
        sigma, silu = mix(gate, up)
        d_gate[s] = (d_act * up * (sigma * (1.0 + gate * (1.0 - sigma)))).astype(BF16)
        d_up[s] = (d_act * silu).astype(BF16)
        return carry

    lax.fori_loop(0, slots, slope, 0)

    def grad(s):
        def body(at):
            terms[0][s, :, at] = dot(d_gate[s], packed[0][:, at], COLS).astype(BF16)
            terms[1][s, :, at] = dot(d_up[s], packed[0][:, at], COLS).astype(BF16)
            terms[2][s, :, at] = dot(act[s], packed[1][:, at], COLS).astype(BF16)

        tiles(body)

    for j in range(1, halves):
        grad(2 * j + 1)
        for i in range(3):
            reduce_near(i, j)
        grad(2 * j)
    for j in range(1, halves):
        for i in range(5):
            reduce_far(i, j)

    def dx_tile(at):
        total = dot(d_gate[0], weights[0][0, :, at]) + dot(d_up[0], weights[1][0, :, at])
        for s in range(1, slots):
            total = total + dot(d_gate[s], weights[0][s, :, at])
            total = total + dot(d_up[s], weights[1][s, :, at])
        put_rows(1, at, total)

    for i in range(3):
        for j in range(1, e_halves):
            ex_near[i, j].wait_recv()
            ex_held[i, j].wait()
            add_rows(e_summed[i].at[j - 1], [e_arrived[i].at[j], e_held[i].at[j]])
            other = lax.rem(e_half + j, e_halves) * 2 + e_side
            ex_far[i, j] = go(
                remote(
                    e_summed[i].at[j - 1],
                    e_landed[i].at[j - 1],
                    ex_fs.at[i, j - 1],
                    ex_fr.at[i, j - 1],
                    "expert",
                    other,
                )
            )
    tiles(dx_tile)
    grad(1)
    for i in range(3):
        reduce_near(i, 0)
    give_back(1)
    grad(0)

    ends = list(sums) + list(hot_sums)
    for i in (3, 4, 0, 1, 2):
        rs_near[i, 0].wait_recv()
        for j in range(1, halves):
            rs_far[i, j].wait_recv()
        add_rows(
            ends[i],
            [arrived[i].at[0], slot_of(locals_[i], 0)]
            + [landed[i].at[j - 1] for j in range(1, halves)],
        )
    for i in range(3):
        ex_near[i, 0].wait_recv()
        ex_held[i, 0].wait()
        for j in range(1, e_halves):
            ex_far[i, j].wait_recv()
        add_rows(
            hot_grads[i],
            [e_arrived[i].at[0], e_held[i].at[0]]
            + [e_landed[i].at[j - 1] for j in range(1, e_halves)],
        )
    for group in (far, near, forwarded, rs_near, rs_far, ex_near, ex_far):
        for copy in group.values():
            copy.wait_send()
    for copy in swaps:
        copy.wait_send()
    for copy in pending:
        copy.wait()


def layer(hot_in, cold_in, own_w, hot_w):
    owners, halves = lax.axis_size("expert"), lax.axis_size("dp") // 2
    e_halves, slots = owners // 2, 2 * halves
    load, width = hot_in[0].shape
    cap = cold_in[0].shape[1]
    units = own_w[0].shape[0]
    rows, part = owners * cap, width // owners
    dma, vmem, shape = pltpu.SemaphoreType.DMA, pltpu.VMEM, jax.ShapeDtypeStruct
    anywhere, inside = pl.BlockSpec(memory_space=pl.ANY), pl.BlockSpec(memory_space=pltpu.VMEM)
    blocks = [(units, width)] * 3 + [(load, width)] * 2
    scratch = [vmem((slots * load, width), BF16)] * 2 + [vmem((slots, units, width), BF16)] * 3
    scratch += [vmem((owners, cap, width), BF16)] * 2 + [vmem((rows, width), BF16)] * 2
    scratch += [vmem((slots, rows, units), F32)] * 2 + [vmem((slots, rows, units), BF16)] * 3
    scratch += [vmem((owners, cap, width), BF16)] * 2 + [vmem((slots, units, width), BF16)] * 3
    scratch += [vmem((slots * load, width), BF16)] * 2 + [vmem((units, width), BF16)] * 3
    scratch += [vmem((halves,) + b, BF16) for b in blocks]
    scratch += [vmem((halves - 1,) + b, BF16) for b in blocks] * 2
    scratch += [vmem((e_halves, units, part), BF16)] * 6
    scratch += [vmem((e_halves - 1, units, part), BF16)] * 6
    scratch += [dma((9,)), dma((5, halves - 1)), dma((5, halves - 1)), dma((5,)), dma((5,))]
    scratch += [dma((5, halves - 1))] * 2 + [dma((2, owners - 1))] * 4
    scratch += [dma((5, halves))] * 2 + [dma((5, halves - 1))] * 2
    scratch += [dma((3, e_halves))] * 2 + [dma((3, e_halves - 1))] * 2 + [dma((3, e_halves))]
    outs = pl.pallas_call(
        layer_kernel,
        out_shape=[shape((owners, cap, width), BF16)] * 2
        + [shape(b, BF16) for b in blocks]
        + [shape((units, part), F32)] * 3,
        in_specs=[anywhere] * 7 + [inside] * 3,
        out_specs=[anywhere] * 2 + [inside] * 8,
        scratch_shapes=scratch,
        compiler_params=pltpu.CompilerParams(
            collective_id=2, has_side_effects=True, vmem_limit_bytes=67043328
        ),
        name="layer",
    )(*hot_in, *cold_in, *own_w, *hot_w)
    return outs[2:], outs[:2]


def local(
    tokens,
    cotangent,
    route_ids,
    route_weights,
    cold_gate,
    cold_up,
    cold_down,
    hot_gate,
    hot_up,
    hot_down,
):
    tok_rows, width = tokens.shape
    top_count = route_ids.shape[1]
    owners = lax.axis_size("expert")
    replicas = lax.axis_size("dp")
    hot_count, hot_units = hot_gate.shape[:2]
    hot_load = tok_rows // 4
    cold_slots = tok_rows * top_count - hot_count * hot_load
    capacity = max(2, 5 * cold_slots // (4 * owners) + 1)
    capacity = (capacity + 7) // 8 * 8
    cold_total = owners * capacity
    hot_rows = hot_count * hot_load
    slot_total = cold_total + hot_rows

    ids_row = route_ids.T
    earlier = lax.broadcasted_iota(jnp.int32, (tok_rows, tok_rows), 0) < lax.broadcasted_iota(
        jnp.int32, (tok_rows, tok_rows), 1
    )
    slots = lax.broadcasted_iota(jnp.int32, (slot_total, tok_rows), 0)
    placing, pieces = [], []
    for k in range(top_count):
        mine = ids_row[k][None, :]
        same = sum((route_ids[:, o][:, None] == mine).astype(jnp.int32) for o in range(top_count))
        rank = jnp.sum(jnp.where(earlier, same, 0), axis=0)[None, :]
        target = jnp.where(
            mine < owners,
            mine * capacity + rank,
            cold_total + (mine - owners) * hot_load + rank,
        )
        hit = slots == target
        placing.append(hit.astype(BF16))
        pieces.append(jnp.where(hit, route_weights[:, k][None, :], 0.0))
    either = sum(placing[1:], placing[0])
    gain = jnp.sum(sum(pieces[1:], pieces[0]), axis=1, keepdims=True)
    send_x = dot(either, tokens).astype(BF16)
    send_d = (gain * dot(either, cotangent)).astype(BF16)

    fits = hot_count == 1 and owners <= 16 and width // owners % 128 == 0
    if fits:
        sums, (back_out, back_dx) = layer(
            (send_x[cold_total:], send_d[cold_total:]),
            (
                send_x[:cold_total].reshape(owners, capacity, width),
                send_d[:cold_total].reshape(owners, capacity, width),
            ),
            (cold_gate[0], cold_up[0], cold_down[0]),
            (hot_gate[0], hot_up[0], hot_down[0]),
        )
    else:
        (g_gate, g_up, g_down, hot_x, hot_d), (cold_x, cold_d) = dispatch(
            (cold_gate[0], cold_up[0], cold_down[0], send_x[cold_total:], send_d[cold_total:]),
            (
                send_x[:cold_total].reshape(owners, capacity, width),
                send_d[:cold_total].reshape(owners, capacity, width),
            ),
        )

        hot_outs, hot_dxs, hot_grads = [], [], []
        for h in range(hot_count):
            rows_x = hot_x[:, h * hot_load : (h + 1) * hot_load].reshape(-1, width)
            rows_d = hot_d[:, h * hot_load : (h + 1) * hot_load].reshape(-1, width)
            out, dx, *grads = expert_block(rows_x, rows_d, hot_gate[h], hot_up[h], hot_down[h])
            hot_outs.append(out.reshape(replicas, hot_load, width))
            hot_dxs.append(dx.reshape(replicas, hot_load, width))
            hot_grads.append(grads)
        hot_out = jnp.concatenate(hot_outs, axis=1)
        hot_dx = jnp.concatenate(hot_dxs, axis=1)
        blocks = [
            jnp.concatenate([grads[m] for grads in hot_grads], axis=0)
            .reshape(hot_count * hot_units, owners, width // owners)
            .transpose(1, 0, 2)
            for m in range(3)
        ]

        out, dx, *terms = expert_block(
            cold_x.reshape(cold_total, width),
            cold_d.reshape(cold_total, width),
            g_gate.reshape(-1, width),
            g_up.reshape(-1, width),
            g_down.reshape(-1, width),
        )
        units = cold_gate.shape[1]
        terms = [term.reshape(replicas, units, width) for term in terms]
        sums, (back_out, back_dx) = combine(
            [("dp", term, BF16) for term in terms]
            + [("dp", hot_out, BF16), ("dp", hot_dx, BF16)]
            + [("expert", block, F32) for block in blocks],
            (out.reshape(owners, capacity, width), dx.reshape(owners, capacity, width)),
        )
    back_outs = jnp.concatenate([back_out.reshape(cold_total, width), sums[3]], axis=0)
    back_grads = jnp.concatenate([back_dx.reshape(cold_total, width), sums[4]], axis=0)
    outs = [dot(p, back_outs, COLS) for p in placing]
    mixed = sum(route_weights[:, k][:, None] * outs[k] for k in range(top_count)).astype(BF16)
    cot = cotangent.astype(F32)
    route_grad = jnp.stack([jnp.sum(cot * o, axis=1) for o in outs], axis=1)
    token_grad = dot(either, back_grads, COLS).astype(BF16)
    hot_sums = [s.reshape(hot_count, hot_units, width // owners) for s in sums[5:]]
    return (mixed, token_grad, route_grad, sums[0][None], sums[1][None], sums[2][None], *hot_sums)


def solution(mesh):
    rows = P(("expert", "dp"), None)
    owned = P("expert", "dp", None)
    hot = P(None, "dp", None)
    hot_out = P(None, "dp", "expert")
    return jax.shard_map(
        local,
        mesh=mesh,
        in_specs=(rows,) * 4 + (owned,) * 3 + (hot,) * 3,
        out_specs=(rows,) * 3 + (owned,) * 3 + (hot_out,) * 3,
        check_vma=False,
    )
```

```python
import functools

import jax
import jax.numpy as jnp
from jax import lax
from jax.experimental import pallas as pl
from jax.experimental.pallas import tpu as pltpu
from jax.sharding import PartitionSpec as P

F32 = jnp.float32
BF16 = jnp.bfloat16
MESH = pl.DeviceIdType.MESH
ROWS = (((1,), (1,)), ((), ()))
COLS = (((0,), (0,)), ((), ()))


def place(axis):
    size = lax.axis_size(axis)
    me = lax.axis_index(axis)
    return me, me // 2, lax.rem(me, 2), size // 2


def remote(src, dst, send, recv, axis, index):
    return pltpu.make_async_remote_copy(
        src_ref=src,
        dst_ref=dst,
        send_sem=send,
        recv_sem=recv,
        device_id={axis: index},
        device_id_type=MESH,
    )


def greet(pairs_axes, all_axes):
    barrier = pltpu.get_barrier_semaphore()
    count = 0
    for axis in pairs_axes:
        me, half, side, halves = place(axis)
        targets = [half * 2 + 1 - side]
        targets += [lax.rem(half + j, halves) * 2 + side for j in range(1, halves)]
        for index in targets:
            pl.semaphore_signal(barrier, inc=1, device_id={axis: index}, device_id_type=MESH)
        count += len(targets)
    for axis in all_axes:
        me, size = lax.axis_index(axis), lax.axis_size(axis)
        for j in range(1, size):
            pl.semaphore_signal(
                barrier, inc=1, device_id={axis: lax.rem(me + j, size)}, device_id_type=MESH
            )
        count += size - 1
    pl.semaphore_wait(barrier, count)


def swap_starts(ins, outs, send, recv):
    me, size = lax.axis_index("expert"), lax.axis_size("expert")
    started = []
    for j in range(1, size):
        for i, (src, dst) in enumerate(zip(ins, outs)):
            other = lax.rem(me + j, size)
            copy = remote(
                src.at[other], dst.at[me], send.at[i, j - 1], recv.at[i, j - 1], "expert", other
            )
            copy.start()
            started.append(copy)
    return started


def dispatch_kernel(gathered, swapped, *refs):
    ag_in, refs = refs[:gathered], refs[gathered:]
    sw_in, refs = refs[:swapped], refs[swapped:]
    ag_out, refs = refs[:gathered], refs[gathered:]
    sw_out, refs = refs[:swapped], refs[swapped:]
    ag_own, refs = refs[:gathered], refs[gathered:]
    sw_own, refs = refs[:swapped], refs[swapped:]
    own_sem, side_send, side_recv, far_send, far_recv, fwd_send, fwd_recv, sw_send, sw_recv = refs
    me, half, side, halves = place("dp")
    rank = lax.axis_index("expert")
    partner = half * 2 + 1 - side
    greet(("dp",), ("expert",))
    far = {}
    for i in range(gathered):
        for j in range(1, halves):
            other = lax.rem(half + j, halves) * 2 + side
            far[i, j] = remote(
                ag_in[i], ag_out[i].at[me], far_send.at[i, j - 1], far_recv.at[i, j - 1], "dp", other
            )
            far[i, j].start()
    swaps = swap_starts(sw_in, sw_out, sw_send, sw_recv)
    sides = []
    for i in range(gathered):
        copy = remote(ag_in[i], ag_out[i].at[me], side_send.at[i], side_recv.at[i], "dp", partner)
        copy.start()
        sides.append(copy)
    loads = []
    for i in range(gathered):
        loads.append((ag_in[i], ag_own[i], ag_out[i].at[me]))
    for i in range(swapped):
        loads.append((sw_in[i].at[rank], sw_own[i], sw_out[i].at[rank]))
    for i, (src, mid, _) in enumerate(loads):
        pltpu.make_async_copy(src, mid, own_sem.at[i]).start()
    for i, (src, mid, dst) in enumerate(loads):
        pltpu.make_async_copy(src, mid, own_sem.at[i]).wait()
        pltpu.make_async_copy(mid, dst, own_sem.at[i]).start()
    forwards = []
    for i in range(gathered):
        for j in range(1, halves):
            far[i, j].wait_recv()
            origin = lax.rem(half + halves - j, halves) * 2 + side
            block = ag_out[i].at[origin]
            copy = remote(
                block, block, fwd_send.at[i, j - 1], fwd_recv.at[i, j - 1], "dp", partner
            )
            copy.start()
            forwards.append(copy)
    for i, (src, mid, dst) in enumerate(loads):
        pltpu.make_async_copy(mid, dst, own_sem.at[i]).wait()
    for copy in far.values():
        copy.wait_send()
    for copy in sides + swaps + forwards:
        copy.wait()


def dispatch(gather, swap):
    ways = lax.axis_size("dp")
    size = lax.axis_size("expert")
    halves = ways // 2
    ng, ns = len(gather), len(swap)
    dma = pltpu.SemaphoreType.DMA
    anywhere = pl.BlockSpec(memory_space=pl.ANY)
    shapes = [jax.ShapeDtypeStruct((ways,) + a.shape, a.dtype) for a in gather]
    shapes += [jax.ShapeDtypeStruct(a.shape, a.dtype) for a in swap]
    outs = pl.pallas_call(
        functools.partial(dispatch_kernel, ng, ns),
        out_shape=shapes,
        in_specs=[anywhere] * (ng + ns),
        out_specs=[anywhere] * (ng + ns),
        scratch_shapes=[pltpu.VMEM(a.shape, a.dtype) for a in gather]
        + [pltpu.VMEM(a.shape[1:], a.dtype) for a in swap]
        + [
            dma((ng + ns,)),
            dma((ng,)),
            dma((ng,)),
            dma((ng, halves - 1)),
            dma((ng, halves - 1)),
            dma((ng, halves - 1)),
            dma((ng, halves - 1)),
            dma((ns, size - 1)),
            dma((ns, size - 1)),
        ],
        compiler_params=pltpu.CompilerParams(
            collective_id=0, has_side_effects=True, vmem_limit_bytes=20 << 20
        ),
        name="dispatch",
    )(*gather, *swap)
    return outs[:ng], outs[ng:]


def add_rows(dst, srcs):
    rows = dst.shape[0]
    step = 16 if rows % 16 == 0 else rows

    def body(i, carry):
        at = pl.ds(pl.multiple_of(i * step, step), step)
        total = srcs[0][at, :].astype(F32)
        for src in srcs[1:]:
            total = total + src[at, :].astype(F32)
        dst[at, :] = total.astype(dst.dtype)
        return carry

    lax.fori_loop(0, rows // step, body, 0)


def combine_kernel(axes, swapped, *refs):
    count = len(axes)
    rs_in, refs = refs[:count], refs[count:]
    sw_in, refs = refs[:swapped], refs[swapped:]
    rs_out, refs = refs[:count], refs[count:]
    sw_out, refs = refs[:swapped], refs[swapped:]
    sw_own, refs = refs[:swapped], refs[swapped:]
    own_sem, sw_send, sw_recv = refs[:3]
    bufs = [refs[3 + 11 * i : 14 + 11 * i] for i in range(count)]
    rank = lax.axis_index("expert")
    greet(("dp",), ("expert",))
    sides, mines = {}, {}
    deepest = max(lax.axis_size(axis) // 2 for axis in axes)
    for turn in range(1, deepest + 1):
        for i, axis in enumerate(axes):
            _, half, side, halves = place(axis)
            if turn > halves:
                continue
            j = turn % halves
            arrived, held, _, _, _, load_sem, s_send, s_recv = bufs[i][:8]
            to = lax.rem(half + j, halves) * 2
            partner = half * 2 + 1 - side
            sides[i, j] = remote(
                rs_in[i].at[to + 1 - side], arrived.at[j], s_send.at[j], s_recv.at[j], axis, partner
            )
            sides[i, j].start()
            mines[i, j] = pltpu.make_async_copy(
                rs_in[i].at[to + side], held.at[j], load_sem.at[j]
            )
            mines[i, j].start()
    swaps = swap_starts(sw_in, sw_out, sw_send, sw_recv)
    for i in range(swapped):
        pltpu.make_async_copy(sw_in[i].at[rank], sw_own[i], own_sem.at[i]).start()
    for i in range(swapped):
        pltpu.make_async_copy(sw_in[i].at[rank], sw_own[i], own_sem.at[i]).wait()
        pltpu.make_async_copy(sw_own[i], sw_out[i].at[rank], own_sem.at[i]).start()
    fars = {}
    for i, axis in enumerate(axes):
        _, half, side, halves = place(axis)
        arrived, held, summed, landed, _, _, _, _, f_send, f_recv, _ = bufs[i]
        for j in range(1, halves):
            sides[i, j].wait_recv()
            mines[i, j].wait()
            add_rows(summed.at[j - 1], [arrived.at[j], held.at[j]])
            other = lax.rem(half + j, halves) * 2 + side
            fars[i, j] = remote(
                summed.at[j - 1], landed.at[j - 1], f_send.at[j - 1], f_recv.at[j - 1], axis, other
            )
            fars[i, j].start()
    puts = []
    for i, axis in enumerate(axes):
        halves = lax.axis_size(axis) // 2
        arrived, held, summed, landed, result, _, _, _, _, _, out_sem = bufs[i]
        sides[i, 0].wait_recv()
        mines[i, 0].wait()
        for j in range(1, halves):
            fars[i, j].wait_recv()
        add_rows(
            result, [arrived.at[0], held.at[0]] + [landed.at[j - 1] for j in range(1, halves)]
        )
        put = pltpu.make_async_copy(result, rs_out[i], out_sem.at[0])
        put.start()
        puts.append(put)
    for i in range(swapped):
        pltpu.make_async_copy(sw_own[i], sw_out[i].at[rank], own_sem.at[i]).wait()
    for copy in list(sides.values()) + list(fars.values()):
        copy.wait_send()
    for copy in swaps + puts:
        copy.wait()


def combine(reduce, swap):
    size = lax.axis_size("expert")
    nr, ns = len(reduce), len(swap)
    dma = pltpu.SemaphoreType.DMA
    anywhere = pl.BlockSpec(memory_space=pl.ANY)
    shapes = [jax.ShapeDtypeStruct(a.shape[1:], kind) for _, a, kind in reduce]
    shapes += [jax.ShapeDtypeStruct(a.shape, a.dtype) for a in swap]
    scratch = [pltpu.VMEM(a.shape[1:], a.dtype) for a in swap]
    scratch += [dma((ns,)), dma((ns, size - 1)), dma((ns, size - 1))]
    for axis, a, kind in reduce:
        halves = lax.axis_size(axis) // 2
        block = a.shape[1:]
        scratch += [
            pltpu.VMEM((halves,) + block, a.dtype),
            pltpu.VMEM((halves,) + block, a.dtype),
            pltpu.VMEM((halves - 1,) + block, a.dtype),
            pltpu.VMEM((halves - 1,) + block, a.dtype),
            pltpu.VMEM(block, kind),
            dma((halves,)),
            dma((halves,)),
            dma((halves,)),
            dma((halves - 1,)),
            dma((halves - 1,)),
            dma((1,)),
        ]
    outs = pl.pallas_call(
        functools.partial(combine_kernel, tuple(axis for axis, _, _ in reduce), ns),
        out_shape=shapes,
        in_specs=[anywhere] * (nr + ns),
        out_specs=[anywhere] * (nr + ns),
        scratch_shapes=scratch,
        compiler_params=pltpu.CompilerParams(
            collective_id=1, has_side_effects=True, vmem_limit_bytes=56 << 20
        ),
        name="combine",
    )(*[a for _, a, _ in reduce], *swap)
    return outs[:nr], outs[nr:]


def dot(a, b, dims=None):
    if dims is None:
        return jnp.dot(a, b, preferred_element_type=F32)
    return lax.dot_general(a, b, dims, preferred_element_type=F32)


def expert_block(rows_x, rows_d, w_gate, w_up, w_down):
    pre_gate = dot(rows_x, w_gate, ROWS)
    pre_up = dot(rows_x, w_up, ROWS)
    sigma = jax.nn.sigmoid(pre_gate)
    act = (pre_gate * sigma * pre_up).astype(BF16)
    out = dot(act, w_down).astype(BF16)
    d_act = dot(rows_d, w_down, ROWS)
    slope = sigma * (1.0 + pre_gate * (1.0 - sigma))
    d_gate = (d_act * pre_up * slope).astype(BF16)
    d_up = (d_act * pre_gate * sigma).astype(BF16)
    dx = (dot(d_gate, w_gate) + dot(d_up, w_up)).astype(BF16)
    return (
        out,
        dx,
        dot(d_gate, rows_x, COLS).astype(BF16),
        dot(d_up, rows_x, COLS).astype(BF16),
        dot(act, rows_d, COLS).astype(BF16),
    )


def mix(pre_gate, pre_up):
    sigma = 1.0 / (1.0 + jnp.exp(-pre_gate))
    return sigma, pre_gate * sigma


def layer_kernel(*refs):
    rows_in, own_w, hot_w = refs[:2], refs[2:5], refs[5:8]
    refs = refs[:2] + refs
    back, sums, hot_sums, hot_grads = refs[10:12], refs[12:15], refs[15:17], refs[17:20]
    hot_rows, weights, landing, packed = refs[20:22], refs[22:25], refs[25:27], refs[27:29]
    pre_g, pre_u, act, d_gate, d_up = refs[29:34]
    results, terms, hot_parts, hot_terms = refs[34:36], refs[36:39], refs[39:41], refs[41:44]
    arrived, summed, landed = refs[44:49], refs[49:54], refs[54:59]
    e_arrived, e_held, e_summed, e_landed = refs[59:62], refs[62:65], refs[65:68], refs[68:71]
    (own_sem, ag_fs, ag_fr, ag_ss, ag_sr, ag_ws, ag_wr, sw_s, sw_r, bk_s, bk_r) = refs[71:82]
    (rs_ss, rs_sr, rs_fs, rs_fr, ex_ss, ex_sr, ex_fs, ex_fr, ex_l) = refs[82:91]
    me, half, side, halves = place("dp")
    rank, e_half, e_side, e_halves = place("expert")
    owners = 2 * e_halves
    partner, e_partner = half * 2 + 1 - side, e_half * 2 + 1 - e_side
    slots = 2 * halves
    cap, width = landing[0].shape[1:]
    load = hot_rows[0].shape[0] // slots
    hot_in = [ref.at[pl.ds(owners * cap, load)] for ref in rows_in]
    part = width // owners
    tile = 512 if width % 512 == 0 else width
    pending = []

    def cold_in(i, index):
        return rows_in[i].at[pl.ds(pl.multiple_of(index * cap, 8), cap)]

    def go(copy):
        copy.start()
        return copy

    def slot_of(buffer, s):
        if len(buffer.shape) == 2:
            return buffer.at[pl.ds(s * load, load)]
        return buffer.at[s]

    def tiles(body):
        def step(i, carry):
            body(pl.ds(pl.multiple_of(i * tile, tile), tile))
            return carry

        lax.fori_loop(0, width // tile, step, 0)

    greet(("dp",), ("expert",))
    sources = list(hot_in) + list(own_w)
    targets = list(hot_rows) + list(weights)
    far, near, forwarded, own = {}, {}, {}, {}

    def send_near(i):
        near[i] = go(
            remote(sources[i], slot_of(targets[i], 1), ag_ss.at[i], ag_sr.at[i], "dp", partner)
        )
        own[i] = go(pltpu.make_async_copy(sources[i], slot_of(targets[i], 0), own_sem.at[i]))

    def forward(i):
        for j in range(1, halves):
            far[i, j].wait_recv()
            forwarded[i, j] = go(
                remote(
                    slot_of(targets[i], 2 * j),
                    slot_of(targets[i], 2 * j + 1),
                    ag_ws.at[i, j - 1],
                    ag_wr.at[i, j - 1],
                    "dp",
                    partner,
                )
            )

    for i in range(5):
        for j in range(1, halves):
            other = lax.rem(half + j, halves) * 2 + side
            far[i, j] = go(
                remote(
                    sources[i],
                    slot_of(targets[i], 2 * j),
                    ag_fs.at[i, j - 1],
                    ag_fr.at[i, j - 1],
                    "dp",
                    other,
                )
            )
    swaps, mine = [], []
    for i in range(2):
        for j in range(1, owners):
            other = lax.rem(rank + j, owners)
            swaps.append(
                go(
                    remote(
                        cold_in(i, other),
                        landing[i].at[rank],
                        sw_s.at[i, j - 1],
                        sw_r.at[i, j - 1],
                        "expert",
                        other,
                    )
                )
            )
        mine.append(
            go(
                pltpu.make_async_copy(
                    cold_in(i, rank), landing[i].at[rank], own_sem.at[5 + i]
                )
            )
        )
    for i in range(5):
        send_near(i)

    for i in (0, 1):
        forward(i)
    for i in (0, 1):
        near[i].wait_recv()
        own[i].wait()
        for j in range(1, halves):
            forwarded[i, j].wait_recv()
    w_gate, w_up, w_down = hot_w
    gate = dot(hot_rows[0][...], w_gate[...], ROWS)
    up = dot(hot_rows[0][...], w_up[...], ROWS)
    sigma, silu = mix(gate, up)
    d_act = dot(hot_rows[1][...], w_down[...], ROWS)
    h_act = (silu * up).astype(BF16)
    h_dg = (d_act * up * (sigma * (1.0 + gate * (1.0 - sigma)))).astype(BF16)
    h_du = (d_act * silu).astype(BF16)

    def hot_tile(at):
        hot_parts[0][:, at] = dot(h_act, w_down[:, at]).astype(BF16)
        hot_parts[1][:, at] = (dot(h_dg, w_gate[:, at]) + dot(h_du, w_up[:, at])).astype(BF16)
        hot_terms[0][:, at] = dot(h_dg, hot_rows[0][:, at], COLS).astype(BF16)
        hot_terms[1][:, at] = dot(h_du, hot_rows[0][:, at], COLS).astype(BF16)
        hot_terms[2][:, at] = dot(h_act, hot_rows[1][:, at], COLS).astype(BF16)

    tiles(hot_tile)

    locals_ = list(terms) + list(hot_parts)
    rs_near, rs_far, ex_near, ex_far, ex_held = {}, {}, {}, {}, {}

    def reduce_near(i, j):
        rs_near[i, j] = go(
            remote(
                slot_of(locals_[i], 2 * j + 1),
                arrived[i].at[j],
                rs_ss.at[i, j],
                rs_sr.at[i, j],
                "dp",
                partner,
            )
        )

    def reduce_far(i, j):
        rs_near[i, j].wait_recv()
        add_rows(summed[i].at[j - 1], [arrived[i].at[j], slot_of(locals_[i], 2 * j)])
        other = lax.rem(half + halves - j, halves) * 2 + side
        rs_far[i, j] = go(
            remote(
                summed[i].at[j - 1],
                landed[i].at[j - 1],
                rs_fs.at[i, j - 1],
                rs_fr.at[i, j - 1],
                "dp",
                other,
            )
        )

    def columns(index):
        return pl.ds(pl.multiple_of(index * part, 128), part)

    quads, quad, turn = e_halves // 2, e_half // 2, lax.rem(e_half, 2)

    def facing(j):
        other = turn if j % 2 == 0 else 1 - turn
        return lax.rem(quad + j // 2, quads) * 2 + other

    for i in range(3):
        for j in list(range(1, e_halves)) + [0]:
            to = facing(j) * 2
            ex_near[i, j] = go(
                remote(
                    hot_terms[i].at[:, columns(to + 1 - e_side)],
                    e_arrived[i].at[j],
                    ex_ss.at[i, j],
                    ex_sr.at[i, j],
                    "expert",
                    e_partner,
                )
            )
            ex_held[i, j] = go(
                pltpu.make_async_copy(
                    hot_terms[i].at[:, columns(to + e_side)], e_held[i].at[j], ex_l.at[i, j]
                )
            )
    for i in (3, 4):
        for j in range(halves - 1, -1, -1):
            reduce_near(i, j)

    def repack(i):
        def step(k, carry):
            a, b = landing[i][2 * k].astype(F32), landing[i][2 * k + 1].astype(F32)
            at = pl.ds(pl.multiple_of(k * 2 * cap, 16), 2 * cap)
            packed[i][at, :] = jnp.concatenate([a, b], axis=0).astype(BF16)
            return carry

        lax.fori_loop(0, owners // 2, step, 0)

    def give_back(i):
        for j in range(1, owners):
            other = lax.rem(rank + j, owners)
            pending.append(
                go(
                    remote(
                        results[i].at[other],
                        back[i].at[rank],
                        bk_s.at[i, j - 1],
                        bk_r.at[i, j - 1],
                        "expert",
                        other,
                    )
                )
            )
        pending.append(
            go(pltpu.make_async_copy(results[i].at[rank], back[i].at[rank], own_sem.at[7 + i]))
        )

    def put_rows(i, at, value):
        for e in range(owners):
            results[i][e, :, at] = value[e * cap : (e + 1) * cap].astype(BF16)

    for copy in swaps[: owners - 1]:
        copy.wait_recv()
    mine[0].wait()
    repack(0)
    for i in (2, 3, 4):
        near[i].wait_recv()
        own[i].wait()

    def project(m, dst, first, last):
        def step(s, carry):
            dst[s] = dot(packed[0][...], weights[m][s], ROWS)
            return carry

        lax.fori_loop(first, last, step, 0)

    project(0, pre_g, 0, 2)
    project(1, pre_u, 0, 2)
    forward(2)
    for j in range(1, halves):
        forwarded[2, j].wait_recv()
    project(0, pre_g, 2, slots)
    forward(3)
    for j in range(1, halves):
        forwarded[3, j].wait_recv()
    project(1, pre_u, 2, slots)

    def cross(i, slot, index):
        return go(
            remote(
                e_summed[i].at[slot],
                e_landed[i].at[slot],
                ex_fs.at[i, slot],
                ex_fr.at[i, slot],
                "expert",
                index * 2 + e_side,
            )
        )

    for i in range(3):
        for k in list(range(1, quads)) + [0]:
            j = 2 * k + 1
            ex_near[i, j].wait_recv()
            ex_held[i, j].wait()
            add_rows(e_summed[i].at[k], [e_arrived[i].at[j], e_held[i].at[j]])
            ex_far[i, k] = cross(i, k, quad * 2 + 1 - turn)

    def activate(s, carry):
        _, silu = mix(pre_g[s], pre_u[s])
        act[s] = (silu * pre_u[s]).astype(BF16)
        return carry

    lax.fori_loop(0, slots, activate, 0)
    forward(4)
    for j in range(1, halves):
        forwarded[4, j].wait_recv()

    def out_tile(at):
        total = dot(act[0], weights[2][0, :, at])
        for s in range(1, slots):
            total = total + dot(act[s], weights[2][s, :, at])
        put_rows(0, at, total)

    tiles(out_tile)

    for copy in swaps[owners - 1 :]:
        copy.wait_recv()
    mine[1].wait()
    give_back(0)
    repack(1)

    def slope(s, carry):
        d_act = dot(packed[1][...], weights[2][s], ROWS)
        gate, up = pre_g[s], pre_u[s]
        sigma, silu = mix(gate, up)
        d_gate[s] = (d_act * up * (sigma * (1.0 + gate * (1.0 - sigma)))).astype(BF16)
        d_up[s] = (d_act * silu).astype(BF16)
        return carry

    lax.fori_loop(0, slots, slope, 0)
    for i in range(3):
        for k in range(1, quads):
            slot, j = quads + k - 1, 2 * k
            ex_near[i, j].wait_recv()
            ex_held[i, j].wait()
            ex_far[i, k].wait_recv()
            add_rows(
                e_summed[i].at[slot], [e_arrived[i].at[j], e_held[i].at[j], e_landed[i].at[k]]
            )
            ex_far[i, slot] = cross(i, slot, facing(j))

    def grad(s):
        def body(at):
            terms[0][s, :, at] = dot(d_gate[s], packed[0][:, at], COLS).astype(BF16)
            terms[1][s, :, at] = dot(d_up[s], packed[0][:, at], COLS).astype(BF16)
            terms[2][s, :, at] = dot(act[s], packed[1][:, at], COLS).astype(BF16)

        tiles(body)

    for j in range(1, halves):
        grad(2 * j + 1)
        for i in range(3):
            reduce_near(i, j)
        grad(2 * j)
    for j in range(1, halves):
        for i in range(5):
            reduce_far(i, j)

    def dx_tile(at):
        total = dot(d_gate[0], weights[0][0, :, at]) + dot(d_up[0], weights[1][0, :, at])
        for s in range(1, slots):
            total = total + dot(d_gate[s], weights[0][s, :, at])
            total = total + dot(d_up[s], weights[1][s, :, at])
        put_rows(1, at, total)

    tiles(dx_tile)
    grad(1)
    for i in range(3):
        reduce_near(i, 0)
    give_back(1)
    grad(0)

    ends = list(sums) + list(hot_sums)
    for i in (3, 4, 0, 1, 2):
        rs_near[i, 0].wait_recv()
        for j in range(1, halves):
            rs_far[i, j].wait_recv()
        add_rows(
            ends[i],
            [arrived[i].at[0], slot_of(locals_[i], 0)]
            + [landed[i].at[j - 1] for j in range(1, halves)],
        )
    for i in range(3):
        ex_near[i, 0].wait_recv()
        ex_held[i, 0].wait()
        got = [slot for slot in range(e_halves - 1) if slot == 0 or slot >= quads]
        for slot in got:
            ex_far[i, slot].wait_recv()
        add_rows(
            hot_grads[i],
            [e_arrived[i].at[0], e_held[i].at[0]] + [e_landed[i].at[slot] for slot in got],
        )
    for group in (far, near, forwarded, rs_near, rs_far, ex_near, ex_far):
        for copy in group.values():
            copy.wait_send()
    for copy in swaps:
        copy.wait_send()
    for copy in pending:
        copy.wait()


def layer(rows_in, cap, load, own_w, hot_w):
    owners, halves = lax.axis_size("expert"), lax.axis_size("dp") // 2
    e_halves, slots = owners // 2, 2 * halves
    width = rows_in[0].shape[1]
    units = own_w[0].shape[0]
    rows, part = owners * cap, width // owners
    dma, vmem, shape = pltpu.SemaphoreType.DMA, pltpu.VMEM, jax.ShapeDtypeStruct
    anywhere, inside = pl.BlockSpec(memory_space=pl.ANY), pl.BlockSpec(memory_space=pltpu.VMEM)
    blocks = [(units, width)] * 3 + [(load, width)] * 2
    scratch = [vmem((slots * load, width), BF16)] * 2 + [vmem((slots, units, width), BF16)] * 3
    scratch += [vmem((owners, cap, width), BF16)] * 2 + [vmem((rows, width), BF16)] * 2
    scratch += [vmem((slots, rows, units), F32)] * 2 + [vmem((slots, rows, units), BF16)] * 3
    scratch += [vmem((owners, cap, width), BF16)] * 2 + [vmem((slots, units, width), BF16)] * 3
    scratch += [vmem((slots * load, width), BF16)] * 2 + [vmem((units, width), BF16)] * 3
    scratch += [vmem((halves,) + b, BF16) for b in blocks]
    scratch += [vmem((halves - 1,) + b, BF16) for b in blocks] * 2
    scratch += [vmem((e_halves, units, part), BF16)] * 6
    scratch += [vmem((e_halves - 1, units, part), BF16)] * 6
    scratch += [dma((9,)), dma((5, halves - 1)), dma((5, halves - 1)), dma((5,)), dma((5,))]
    scratch += [dma((5, halves - 1))] * 2 + [dma((2, owners - 1))] * 4
    scratch += [dma((5, halves))] * 2 + [dma((5, halves - 1))] * 2
    scratch += [dma((3, e_halves))] * 2 + [dma((3, e_halves - 1))] * 2 + [dma((3, e_halves))]
    outs = pl.pallas_call(
        layer_kernel,
        out_shape=[shape((owners, cap, width), BF16)] * 2
        + [shape(b, BF16) for b in blocks]
        + [shape((units, part), F32)] * 3,
        in_specs=[anywhere] * 5 + [inside] * 3,
        out_specs=[anywhere] * 2 + [inside] * 8,
        scratch_shapes=scratch,
        compiler_params=pltpu.CompilerParams(
            collective_id=2, has_side_effects=True, vmem_limit_bytes=67043328
        ),
        name="layer",
    )(*rows_in, *own_w, *hot_w)
    return outs[2:], outs[:2]


def local(
    tokens,
    cotangent,
    route_ids,
    route_weights,
    cold_gate,
    cold_up,
    cold_down,
    hot_gate,
    hot_up,
    hot_down,
):
    tok_rows, width = tokens.shape
    top_count = route_ids.shape[1]
    owners = lax.axis_size("expert")
    replicas = lax.axis_size("dp")
    hot_count, hot_units = hot_gate.shape[:2]
    hot_load = tok_rows // 4
    cold_slots = tok_rows * top_count - hot_count * hot_load
    capacity = max(2, 5 * cold_slots // (4 * owners) + 1)
    capacity = (capacity + 7) // 8 * 8
    cold_total = owners * capacity
    hot_rows = hot_count * hot_load
    slot_total = cold_total + hot_rows

    ids_row = route_ids.T
    earlier = lax.broadcasted_iota(jnp.int32, (tok_rows, tok_rows), 0) < lax.broadcasted_iota(
        jnp.int32, (tok_rows, tok_rows), 1
    )
    slots = lax.broadcasted_iota(jnp.int32, (slot_total, tok_rows), 0)
    placing, pieces = [], []
    for k in range(top_count):
        mine = ids_row[k][None, :]
        same = sum((route_ids[:, o][:, None] == mine).astype(jnp.int32) for o in range(top_count))
        rank = jnp.sum(jnp.where(earlier, same, 0), axis=0)[None, :]
        target = jnp.where(
            mine < owners,
            mine * capacity + rank,
            cold_total + (mine - owners) * hot_load + rank,
        )
        hit = slots == target
        placing.append(hit.astype(BF16))
        pieces.append(jnp.where(hit, route_weights[:, k][None, :], 0.0))
    either = sum(placing[1:], placing[0])
    gain = jnp.sum(sum(pieces[1:], pieces[0]), axis=1, keepdims=True)
    send_x = dot(either, tokens).astype(BF16)
    send_d = (gain * dot(either, cotangent)).astype(BF16)

    fits = hot_count == 1 and owners % 4 == 0 and owners <= 16 and width // owners % 128 == 0
    if fits:
        sums, (back_out, back_dx) = layer(
            (send_x, send_d),
            capacity,
            hot_load,
            (cold_gate[0], cold_up[0], cold_down[0]),
            (hot_gate[0], hot_up[0], hot_down[0]),
        )
    else:
        (g_gate, g_up, g_down, hot_x, hot_d), (cold_x, cold_d) = dispatch(
            (cold_gate[0], cold_up[0], cold_down[0], send_x[cold_total:], send_d[cold_total:]),
            (
                send_x[:cold_total].reshape(owners, capacity, width),
                send_d[:cold_total].reshape(owners, capacity, width),
            ),
        )

        hot_outs, hot_dxs, hot_grads = [], [], []
        for h in range(hot_count):
            rows_x = hot_x[:, h * hot_load : (h + 1) * hot_load].reshape(-1, width)
            rows_d = hot_d[:, h * hot_load : (h + 1) * hot_load].reshape(-1, width)
            out, dx, *grads = expert_block(rows_x, rows_d, hot_gate[h], hot_up[h], hot_down[h])
            hot_outs.append(out.reshape(replicas, hot_load, width))
            hot_dxs.append(dx.reshape(replicas, hot_load, width))
            hot_grads.append(grads)
        hot_out = jnp.concatenate(hot_outs, axis=1)
        hot_dx = jnp.concatenate(hot_dxs, axis=1)
        blocks = [
            jnp.concatenate([grads[m] for grads in hot_grads], axis=0)
            .reshape(hot_count * hot_units, owners, width // owners)
            .transpose(1, 0, 2)
            for m in range(3)
        ]

        out, dx, *terms = expert_block(
            cold_x.reshape(cold_total, width),
            cold_d.reshape(cold_total, width),
            g_gate.reshape(-1, width),
            g_up.reshape(-1, width),
            g_down.reshape(-1, width),
        )
        units = cold_gate.shape[1]
        terms = [term.reshape(replicas, units, width) for term in terms]
        sums, (back_out, back_dx) = combine(
            [("dp", term, BF16) for term in terms]
            + [("dp", hot_out, BF16), ("dp", hot_dx, BF16)]
            + [("expert", block, F32) for block in blocks],
            (out.reshape(owners, capacity, width), dx.reshape(owners, capacity, width)),
        )
    back_outs = jnp.concatenate([back_out.reshape(cold_total, width), sums[3]], axis=0)
    back_grads = jnp.concatenate([back_dx.reshape(cold_total, width), sums[4]], axis=0)
    outs = [dot(p, back_outs, COLS) for p in placing]
    mixed = sum(route_weights[:, k][:, None] * outs[k] for k in range(top_count)).astype(BF16)
    cot = cotangent.astype(F32)
    route_grad = jnp.stack([jnp.sum(cot * o, axis=1) for o in outs], axis=1)
    token_grad = dot(either, back_grads, COLS).astype(BF16)
    hot_sums = [s.reshape(hot_count, hot_units, width // owners) for s in sums[5:]]
    return (mixed, token_grad, route_grad, sums[0][None], sums[1][None], sums[2][None], *hot_sums)


def solution(mesh):
    rows = P(("expert", "dp"), None)
    owned = P("expert", "dp", None)
    hot = P(None, "dp", None)
    hot_out = P(None, "dp", "expert")
    return jax.shard_map(
        local,
        mesh=mesh,
        in_specs=(rows,) * 4 + (owned,) * 3 + (hot,) * 3,
        out_specs=(rows,) * 3 + (owned,) * 3 + (hot_out,) * 3,
        check_vma=False,
    )
```
